32 devices in a mesh: dp: 16 (over z, y, core), tensor: 2 (over x).
Axes of the slice: x: 2, y: 2, z: 4, core: 2. Of those that a mesh axis runs over, the one named last changes fastest.
Arguments:
- tokens: bfloat16 [2, 9456, 768], P(None, 'dp'), may hold values from -6 to 6
- segment: int32 [2, 9456], P(None, 'dp'), may hold values from 0 to 3, as said below
- cotangent: bfloat16 [2, 9456, 768], P(None, 'dp'), may hold values from -6 to 6
- ln_gain: float32 [2, 768], replicated, may hold values from 0.5 to 1.5
- ln_shift: float32 [2, 768], replicated, may hold values from -1.8 to 1.8
- qkv_weight: bfloat16 [3, 768, 768], P(None, 'dp', 'tensor'), may hold values from -0.21875 to 0.21875
- qv_bias: float32 [2, 768], P(None, 'tensor'), may hold values from -1.8 to 1.8
- out_weight: bfloat16 [768, 768], P('tensor', 'dp'), may hold values from -2.5 to 2.5
- out_bias: float32 [2, 768], replicated, may hold values from -1.8 to 1.8
- layer_scale: float32 [2, 768], replicated, may hold values from 0.5 to 1.5
- up_weight: bfloat16 [768, 3072], P('dp', 'tensor'), may hold values from -0.21875 to 0.21875
- up_bias: float32 [3072], P('tensor'), may hold values from -1.8 to 1.8
- down_weight: bfloat16 [3072, 768], P('tensor', 'dp'), may hold values from -0.109375 to 0.109375
Outputs:
- block_output: bfloat16 [2, 9456, 768], P(None, 'dp')
- input_grad: bfloat16 [2, 9456, 768], P(None, 'dp')
- ln_gain_grad: float32 [2, 768], replicated
- ln_shift_grad: float32 [2, 768], replicated
- qkv_grad: float32 [3, 768, 768], P(None, 'dp', 'tensor')
- qv_bias_grad: float32 [2, 768], P(None, 'tensor')
- out_weight_grad: float32 [768, 768], P('tensor', 'dp')
- out_bias_grad: float32 [2, 768], replicated
- layer_scale_grad: float32 [2, 768], replicated
- up_grad: float32 [768, 3072], P('dp', 'tensor')
- up_bias_grad: float32 [3072], P('tensor')
- down_grad: float32 [3072, 768], P('tensor', 'dp')
The draws below stay inside these ranges and needn't reach their ends.
Inputs may be any that keep to these rules, and one draw needn't show every extreme that they name: `segment`: within each micro-batch, each device's block of 591 positions holds either three images of 197 patches (position p belongs to image p // 197) or one image of 577 patches (image 0) followed by padding numbered 3; the second layout falls on 6 devices (at least one) of each micro-batch, drawn from the seed.
All inputs are finite; a program needn't handle non-finite values.
Results may differ from the reference program's by a relative error of at most 0.015.
Values may be sent and summed in bfloat16 or wider, within the bound.
No kernel may reach another device: no remote copies, remote signals or barrier semaphores. Data moves between devices by JAX's collectives and lax.ppermute only.
A program may use at most 128 MiB of HBM per device.

```python
import jax
import jax.numpy as jnp
from jax import lax

D = 768
HEADS = 12
FF = 3072
SMALL_IMG = 197
LARGE_IMG = 577
MB = 2
CAP = 591
TOKENS = 9456
N_TENSOR = 2


def draw_segment(key, part):
    device_count = TOKENS // CAP
    chosen = max(1, 3 * device_count // 8)
    keys_all = jax.random.split(key, MB)
    orders = jax.vmap(lambda one_key: jax.random.permutation(one_key, device_count))(keys_all)
    large_layout = orders < chosen
    position = jnp.arange(CAP, dtype=jnp.int32)
    small_labels = position // SMALL_IMG
    large_labels = jnp.where(position < LARGE_IMG, 0, 3).astype(jnp.int32)
    labels = jnp.where(large_layout[:, :, None], large_labels[None, None, :], small_labels[None, None, :])
    return labels.reshape(MB, TOKENS).astype(jnp.int32)


def strengthened(values, stream_key, source, target, shards_of, factor):
    def block_of(dim):
        return (jnp.arange(values.shape[dim]) // (values.shape[dim] // shards_of)).reshape((-1,) + (1,) * (values.ndim - 1 - dim))

    near = jax.random.permutation(stream_key, shards_of)[block_of(target)]
    second = (block_of(target) + shards_of // 2) % shards_of
    return jnp.where((block_of(source) == near) | (block_of(source) == second), factor * values, values)


def shard_levels(key, dims, shards, least, largest):
    loudness, own = 1.0, jax.random.fold_in(key, 6)
    for dim, shards_of in shards:
        heights = jnp.exp(jax.random.uniform(jax.random.fold_in(own, dim), (shards_of,), jnp.float32, least / len(shards), largest / len(shards)))
        loudness = loudness * jnp.repeat(heights, dims[dim] // shards_of).reshape([-1 if axis == dim else 1 for axis in range(len(dims))])
    return loudness


def noise(rng, dims, scale, most, cuts=(), kind=jnp.bfloat16):
    drawn = scale * jax.random.normal(rng, dims, jnp.float32)
    if cuts:
        drawn = drawn * shard_levels(rng, dims, cuts, -0.22, 0.18)
    return jnp.clip(drawn, -most, most).astype(kind)


def gaussian_with(rng, dims, scale, limit, cuts, heavy, kind=jnp.bfloat16):
    array = scale * jax.random.normal(rng, dims, jnp.float32)
    if cuts:
        array = array * shard_levels(rng, dims, cuts, -0.22, 0.18)
    return jnp.clip(strengthened(array, jax.random.fold_in(rng, 3), *heavy), -limit, limit).astype(kind)


def setup_inputs(seed: int = 0) -> dict:
    seeds = jax.random.split(jax.random.key(seed), 14)
    return {
        "tokens": gaussian_with(seeds[0], (MB, TOKENS, D), 1.0, 6.0, ((1, 16),), (1, 2, 16, 2.0)),
        "segment": draw_segment(jax.random.fold_in(seeds[13], 71), 0),
        "cotangent": gaussian_with(seeds[2], (MB, TOKENS, D), 1.0, 6.0, ((1, 16),), (1, 2, 16, 2.0)),
        "ln_gain": jnp.clip(1.0 + 0.1 * jax.random.normal(seeds[3], (2, D), jnp.float32), 0.5, 1.5),
        "ln_shift": noise(seeds[4], (2, D), 0.3, 1.8, (), jnp.float32),
        "qkv_weight": noise(seeds[5], (3, D, D), D ** -0.5, 0.21875, ((1, 16), (2, 2))),
        "qv_bias": noise(seeds[6], (2, D), 0.3, 1.8, ((1, 2),), jnp.float32),
        "out_weight": noise(seeds[7], (D, D), (max(D // 128, 4)) ** -0.5, 2.5, ((0, 2), (1, 16))),
        "out_bias": noise(seeds[8], (2, D), 0.3, 1.8, (), jnp.float32),
        "layer_scale": jnp.clip(jax.random.uniform(seeds[9], (2, D), jnp.float32, 0.5, 1.5), 0.5, 1.5),
        "up_weight": noise(seeds[10], (D, FF), D ** -0.5, 0.21875, ((0, 16), (1, 2))),
        "up_bias": noise(seeds[11], (FF,), 0.3, 1.8, ((0, 2),), jnp.float32),
        "down_weight": noise(seeds[12], (FF, D), FF ** -0.5, 0.109375, ((0, 2), (1, 16))),
    }


epsilon = 1e-06
padding_id = 3
masked_score = -1e+30

@jax.custom_vjp
def low(v):
    return lax.optimization_barrier(v.astype(jnp.bfloat16)).astype(jnp.float32)

@jax.custom_vjp
def low_back(v):
    return v

def low_keep(v):
    return (low(v), None)

def low_pass(kept, grad):
    return (grad,)

def back_keep(v):
    return (v, None)

def back_low(kept, grad):
    return (low(grad),)
low.defvjp(low_keep, low_pass)
low_back.defvjp(back_keep, back_low)

def dot_highest(left_side, right_side):
    return jnp.dot(left_side, right_side, precision=lax.Precision.HIGHEST, preferred_element_type=jnp.float32)

def layer_norm(inputs, norm_gain, norm_shift):
    center = inputs - lax.optimization_barrier(jnp.mean(inputs, axis=-1, keepdims=True))
    spread = lax.optimization_barrier(jnp.mean(center * center, axis=-1, keepdims=True))
    return center * lax.rsqrt(spread + epsilon) * norm_gain + norm_shift

def split_product(left_side, right_side):
    share_width = left_side.shape[1] // N_TENSOR
    summed = jnp.zeros((left_side.shape[0], right_side.shape[1]), jnp.float32)
    for tensor_rank in range(N_TENSOR):
        lower = tensor_rank * share_width
        upper = lower + share_width
        summed = summed + low(dot_highest(left_side[:, lower:upper], right_side[lower:upper]))
    return summed

def one_block(token_rows, labels, params):
    ln_gain, ln_shift, qkv_weight, qv_bias, out_weight, out_bias, layer_scale, up_weight, up_bias, down_weight = params
    head_size = D // HEADS
    score_scale = head_size ** (-0.5)
    row_count = token_rows.shape[0]
    normed_one = low(layer_norm(token_rows, ln_gain[0], ln_shift[0]))
    queries = low_back(low(dot_highest(normed_one, qkv_weight[0]) + qv_bias[0])).reshape(row_count, HEADS, head_size)
    key_heads = low_back(low(dot_highest(normed_one, qkv_weight[1]))).reshape(row_count, HEADS, head_size)
    value_heads = low_back(low(dot_highest(normed_one, qkv_weight[2]) + qv_bias[1])).reshape(row_count, HEADS, head_size)
    raw_scores = jnp.einsum('qhd,khd->hqk', queries, key_heads, precision=lax.Precision.HIGHEST)
    same_image = labels[:, None] == labels[None, :]
    scores = low_back(jnp.where(same_image[None], raw_scores * score_scale, masked_score))
    probs = jax.nn.softmax(scores, axis=-1)
    mixed_heads = jnp.einsum('hqk,khd->qhd', low(probs), value_heads, precision=lax.Precision.HIGHEST)
    mixed_heads = low_back(low(mixed_heads)).reshape(row_count, D)
    attended = low_back(split_product(mixed_heads, out_weight)) + out_bias[0]
    middle = token_rows + layer_scale[0] * attended
    normed_two = low(layer_norm(middle, ln_gain[1], ln_shift[1]))
    hidden = low_back(dot_highest(normed_two, up_weight) + up_bias)
    activated = low(jax.nn.gelu(hidden, approximate=False))
    ffn_out = low_back(split_product(activated, down_weight)) + out_bias[1]
    return middle + layer_scale[1] * ffn_out

def forward(token_rows, params, labels):
    blocks = token_rows.reshape(-1, CAP, D)
    label_blocks = labels.reshape(-1, CAP)
    block_fn = jax.checkpoint(lambda block_pair: one_block(block_pair[0], block_pair[1], params))
    return lax.map(block_fn, (blocks, label_blocks)).reshape(token_rows.shape)

def reference(tokens, segment, cotangent, ln_gain, ln_shift, qkv_weight, qv_bias, out_weight, out_bias, layer_scale, up_weight, up_bias, down_weight):
    params = tuple((source_array.astype(jnp.float32) for source_array in (ln_gain, ln_shift, qkv_weight, qv_bias, out_weight, out_bias, layer_scale, up_weight, up_bias, down_weight)))
    token_rows = tokens.astype(jnp.float32)
    live = (segment != padding_id).astype(jnp.float32)[..., None]

    def closed(rows_in, params_in):
        return forward(rows_in, params_in, segment)
    result, pullback = jax.vjp(closed, token_rows, params)
    grad_rows, grad_params = pullback(cotangent.astype(jnp.float32) * live)
    return (result.astype(jnp.bfloat16), grad_rows.astype(jnp.bfloat16), grad_params[0], grad_params[1], grad_params[2], grad_params[3], grad_params[4], grad_params[5], grad_params[6], grad_params[7], grad_params[8], grad_params[9])
```

```python
import jax
import jax.numpy as jnp
from jax import lax
from jax.sharding import PartitionSpec as P

HEAD = 64
epsilon = 1e-06
padding_id = 3
masked_score = -1e30
BF = jnp.bfloat16
F32 = jnp.float32
BOTH = ("dp", "tensor")
CHIPS = 8


def dot(a, b, ca, cb):
    return lax.dot_general(a, b, (((ca,), (cb,)), ((), ())), preferred_element_type=F32)


def norm(v):
    center = v - jnp.mean(v, axis=-1, keepdims=True)
    inv = lax.rsqrt(jnp.mean(center * center, axis=-1, keepdims=True) + epsilon)
    return center * inv, inv


def norm_back(grad, unit, inv, gain):
    g = grad * gain
    return inv * (
        g
        - jnp.mean(g, axis=-1, keepdims=True)
        - unit * jnp.mean(g * unit, axis=-1, keepdims=True)
    )


def chip_at(pos):
    pos = lax.rem(pos + 2 * CHIPS, CHIPS)
    return jnp.where(pos < 4, 2 * pos, 15 - 2 * pos)


def pos_of(chip):
    z, y = chip // 2, chip % 2
    return jnp.where(y == 0, z, 7 - z)


RING = [0, 2, 4, 6, 7, 5, 3, 1]


def ring_perm(step):
    pairs = []
    for p in range(CHIPS):
        a, b = RING[p], RING[(p + step) % CHIPS]
        pairs += [(2 * a, 2 * b), (2 * a + 1, 2 * b + 1)]
    return pairs


CW, CCW = ring_perm(1), ring_perm(-1)
SWAP_CORE = [(i, i ^ 1) for i in range(2 * CHIPS)]


def pair_perm(table):
    return [
        (z * 4 + a[0] * 2 + a[1], z * 4 + b[0] * 2 + b[1])
        for z in range(CHIPS)
        for a, b in table
    ]


SPREAD_A = pair_perm(
    [((1, 1), (1, 0)), ((0, 0), (0, 1)), ((1, 0), (0, 0)), ((0, 1), (1, 1))]
)
COLLECT_A = [(b, a) for a, b in SPREAD_A]
CROSS = pair_perm([((0, 1), (1, 0)), ((1, 0), (0, 1))])


class Ring:
    def __init__(self):
        d = lax.axis_index("dp")
        self.core = d % 2
        self.t = lax.axis_index("tensor")
        self.same = self.t == self.core
        self.chip = d // 2
        self.pos = pos_of(self.chip)
        self.first = self.core

    def gather(self, shard):
        rows, cols = shard.shape
        a = lax.ppermute(shard, BOTH, SPREAD_A)
        b = lax.ppermute(shard, BOTH, CROSS)
        mine = jnp.where(self.same, shard, a)
        other = jnp.where(self.same, a, b)
        low = self.core == 0
        block = jnp.stack([jnp.where(low, mine, other), jnp.where(low, other, mine)])
        block = block.reshape(1, 2 * rows, cols)
        full = jnp.zeros((CHIPS, 2 * rows, cols), shard.dtype)
        full = lax.dynamic_update_slice_in_dim(full, block, self.chip, 0)
        up = down = block
        for step in range(1, 5):
            up = lax.ppermute(up, "dp", CW)
            full = lax.dynamic_update_slice_in_dim(full, up, chip_at(self.pos - step), 0)
            if step < 4:
                down = lax.ppermute(down, "dp", CCW)
                full = lax.dynamic_update_slice_in_dim(full, down, chip_at(self.pos + step), 0)
        full = full.reshape(CHIPS * 2 * rows, cols)
        return full, lax.ppermute(full, "dp", SWAP_CORE)

    def reduce(self, own, partner):
        rows, cols = own.shape
        came = lax.ppermute(partner.astype(BF), "dp", SWAP_CORE)
        own = own.reshape(CHIPS, rows // CHIPS, cols)
        came = came.reshape(CHIPS, rows // CHIPS, cols)

        def local(pos):
            at = chip_at(pos)
            return lax.dynamic_index_in_dim(own, at, 0, False).astype(
                F32
            ) + lax.dynamic_index_in_dim(came, at, 0, False).astype(F32)

        up = lax.ppermute(local(self.pos + 4).astype(BF), "dp", CW)
        down = lax.ppermute(local(self.pos - 3).astype(BF), "dp", CCW)
        for k in (3, 2, 1):
            up = lax.ppermute((local(self.pos + k) + up.astype(F32)).astype(BF), "dp", CW)
            if k < 3:
                down = lax.ppermute((local(self.pos - k) + down.astype(F32)).astype(BF), "dp", CCW)
        total = local(self.pos) + up.astype(F32) + down.astype(F32)
        total = total.reshape(2, rows // (2 * CHIPS), cols)
        mine = lax.dynamic_index_in_dim(total, self.core, 0, False)
        other = lax.dynamic_index_in_dim(total, 1 - self.core, 0, False)
        a = lax.ppermute(jnp.where(self.same, other, mine).astype(BF), BOTH, COLLECT_A)
        b = lax.ppermute(other.astype(BF), BOTH, CROSS)
        return jnp.where(self.same, mine, b.astype(F32)) + a.astype(F32)

    def total(self, vector):
        for bit in (2, 1, 4, 8, 16):
            vector = vector + lax.ppermute(vector, BOTH, [(i, i ^ bit) for i in range(32)])
        return vector


class Native:
    first = 0

    def __init__(self):
        self.t = lax.axis_index("tensor")

    def gather(self, shard):
        full = lax.all_gather(shard, "dp", axis=0, tiled=True)
        both = lax.all_gather(full, "tensor", axis=0)
        return both[0], both[1]

    def reduce(self, own, partner):
        both = jnp.stack([own, partner]).astype(F32)
        half = lax.psum_scatter(both, "tensor", scatter_dimension=0)
        return lax.psum_scatter(half, "dp", scatter_dimension=0, tiled=True)

    def total(self, vector):
        return lax.psum(vector, BOTH)


def on_device(
    ring,
    tokens,
    segment,
    cotangent,
    ln_gain,
    ln_shift,
    qkv_weight,
    qv_bias,
    out_weight,
    out_bias,
    layer_scale,
    up_weight,
    up_bias,
    down_weight,
):
    net = Ring() if ring else Native()
    t = net.t
    first = net.first
    swap = [(0, 1), (1, 0)]
    rows, width = tokens.shape[1:]
    shard = qkv_weight.shape[1]
    half = qkv_weight.shape[2]
    heads = half // HEAD
    scale = HEAD**-0.5

    qkv = net.gather(qkv_weight.transpose(1, 0, 2).reshape(shard, 3 * half))
    bias_own = jnp.concatenate([qv_bias.reshape(-1), up_bias])
    bias_far = lax.ppermute(bias_own, "tensor", swap)
    match = t == first
    bias = (jnp.where(match, bias_own, bias_far), jnp.where(match, bias_far, bias_own))
    out_t = net.gather(out_weight.T)
    up = net.gather(up_weight)
    down_t = net.gather(down_weight.T)

    x = lax.dynamic_index_in_dim(tokens, t, 0, False).astype(F32)
    labels = lax.dynamic_index_in_dim(segment, t, 0, False)
    dy = lax.dynamic_index_in_dim(cotangent, t, 0, False).astype(F32)
    dy = dy * (labels != padding_id).astype(F32)[:, None]

    unit1, inv1 = norm(x)
    n1 = (unit1 * ln_gain[0] + ln_shift[0]).astype(BF)
    same_image = labels[:, None] == labels[None, :]

    def split(v):
        return v.astype(BF).reshape(rows, heads, HEAD)

    def scores_of(q, k):
        raw = jnp.einsum("qhd,khd->hqk", q, k, preferred_element_type=F32)
        return jnp.where(same_image[None], raw * scale, masked_score)

    kept = []
    attended = out_bias[0]
    for i in range(2):
        proj = dot(n1, qkv[i], 1, 0)
        q = split(proj[:, :half] + bias[i][:half])
        k = split(proj[:, half : 2 * half])
        v = split(proj[:, 2 * half :] + bias[i][half : 2 * half])
        s = scores_of(q, k)
        top = jnp.max(s, axis=-1, keepdims=True)
        lse = top + jnp.log(jnp.sum(jnp.exp(s - top), axis=-1, keepdims=True))
        p = jnp.exp(s - lse).astype(BF)
        o = jnp.einsum("hqk,khd->qhd", p, v, preferred_element_type=F32)
        o = o.astype(BF).reshape(rows, half)
        kept.append((q, k, v, lse, o))
        attended = attended + dot(o, out_t[i], 1, 1).astype(BF).astype(F32)
    x1 = x + layer_scale[0] * attended
    unit2, inv2 = norm(x1)
    n2 = (unit2 * ln_gain[1] + ln_shift[1]).astype(BF)
    df = dy * layer_scale[1]
    dfr = df.astype(BF)

    ffo = out_bias[1]
    dn2 = 0.0
    up_grads, down_grads, up_bias_grads = [], [], []
    for i in range(2):
        hid = dot(n2, up[i], 1, 0) + bias[i][2 * half :]
        act, pull = jax.vjp(lambda h: jax.nn.gelu(h, approximate=False), hid)
        g = act.astype(BF)
        ffo = ffo + dot(g, down_t[i], 1, 1).astype(BF).astype(F32)
        dh = pull(dot(dfr, down_t[i], 1, 0))[0].astype(BF)
        dn2 = dn2 + dot(dh, up[i], 1, 1)
        up_bias_grads.append(jnp.sum(dh.astype(F32), axis=0))
        up_grads.append(dot(n2, dh, 0, 0).astype(BF))
        down_grads.append(dot(dfr, g, 0, 0).astype(BF))
    up_grad = net.reduce(*up_grads)
    down_grad = net.reduce(*down_grads).T
    result = (x1 + layer_scale[1] * ffo).astype(BF)
    result_far = lax.ppermute(result, "tensor", swap)

    dx1 = dy + norm_back(dn2, unit2, inv2, ln_gain[1])
    da = dx1 * layer_scale[0]
    dar = da.astype(BF)

    dn1 = 0.0
    out_grads, qkv_grads, q_bias_grads, v_bias_grads = [], [], [], []
    for i in range(2):
        q, k, v, lse, o = kept[i]
        out_grads.append(dot(dar, o, 0, 0).astype(BF))
        do = split(dot(dar, out_t[i], 1, 0))
        p = jnp.exp(scores_of(q, k) - lse)
        dp = jnp.einsum("qhd,khd->hqk", do, v, preferred_element_type=F32)
        dv = jnp.einsum("hqk,qhd->khd", p.astype(BF), do, preferred_element_type=F32)
        ds = (p * (dp - jnp.sum(p * dp, axis=-1, keepdims=True))).astype(BF)
        dq = jnp.einsum("hqk,khd->qhd", ds, k, preferred_element_type=F32) * scale
        dk = jnp.einsum("hqk,qhd->khd", ds, q, preferred_element_type=F32) * scale
        dqkv = [v_.astype(BF).reshape(rows, half) for v_ in (dq, dk, dv)]
        q_bias_grads.append(jnp.sum(dqkv[0].astype(F32), axis=0))
        v_bias_grads.append(jnp.sum(dqkv[2].astype(F32), axis=0))
        dqkv = jnp.concatenate(dqkv, axis=1)
        qkv_grads.append(dot(n1, dqkv, 0, 0).astype(BF))
        dn1 = dn1 + dot(dqkv, qkv[i], 1, 1)
    out_grad = net.reduce(*out_grads).T
    qkv_grad = net.reduce(*qkv_grads).reshape(shard, 3, half).transpose(1, 0, 2)
    input_grad = (dx1 + norm_back(dn1, unit1, inv1, ln_gain[0])).astype(BF)
    input_far = lax.ppermute(input_grad, "tensor", swap)

    def ordered(pair):
        if isinstance(first, int):
            return jnp.concatenate(pair)
        a, b = pair
        return jnp.where(
            first == 0, jnp.concatenate([a, b]), jnp.concatenate([b, a])
        )

    vectors = [
        jnp.sum(dn1 * unit1, axis=0),
        jnp.sum(dn2 * unit2, axis=0),
        jnp.sum(dn1, axis=0),
        jnp.sum(dn2, axis=0),
        jnp.sum(da, axis=0),
        jnp.sum(df, axis=0),
        jnp.sum(dx1 * attended, axis=0),
        jnp.sum(dy * ffo, axis=0),
        ordered(q_bias_grads),
        ordered(v_bias_grads),
        ordered(up_bias_grads),
    ]
    sums = net.total(jnp.concatenate(vectors))
    small = sums[: 10 * width].reshape(5, 2, width)
    tensor_half = lambda v, size: lax.dynamic_slice_in_dim(v, t * size, size, v.ndim - 1)

    def both(own, far):
        return jnp.where(t == 0, jnp.stack([own, far]), jnp.stack([far, own]))

    return (
        both(result, result_far),
        both(input_grad, input_far),
        small[0],
        small[1],
        qkv_grad,
        tensor_half(small[4], half),
        out_grad,
        small[2],
        small[3],
        up_grad,
        tensor_half(sums[10 * width :], up_bias.shape[0]),
        down_grad,
    )


def solution(mesh):
    ring = mesh.shape["dp"] == 2 * CHIPS and mesh.shape["tensor"] == 2
    rows3 = P(None, "dp", None)
    placed = (
        rows3,
        P(None, "dp"),
        rows3,
        P(),
        P(),
        P(None, "dp", "tensor"),
        P(None, "tensor"),
        P("tensor", "dp"),
        P(),
        P(),
        P("dp", "tensor"),
        P("tensor"),
        P("tensor", "dp"),
    )
    return jax.shard_map(
        lambda *args: on_device(ring, *args),
        mesh=mesh,
        in_specs=placed,
        out_specs=(
            rows3,
            rows3,
            P(),
            P(),
            P(None, "dp", "tensor"),
            P(None, "tensor"),
            P("tensor", "dp"),
            P(),
            P(),
            P("dp", "tensor"),
            P("tensor"),
            P("tensor", "dp"),
        ),
        check_vma=False,
    )
```
